256 devices in a mesh: row: 16 (over x, y), col: 16 (over z, core).
Axes of the slice: x: 4, y: 4, z: 8, core: 2. Of those that a mesh axis runs over, the one named last changes fastest.
Arguments:
- queries: bfloat16 [4096, 8192], P('col', 'row'), may hold values from -1 to 1
- passages: bfloat16 [4096, 8192], P('row', 'col'), may hold values from -1 to 1
- ce_scores: float32 [8192, 8192], P('row', 'col'), may hold values from -16 to 320
- colbert_scores: float32 [8192, 8192], P('row', 'col'), may hold values from -16 to 320
- mix: int32 [8192], P('row'), may hold values from 1 to 255
- positive: int32 [8192], P('row'), may hold values from 0 to 8191
Outputs:
- query_grad: bfloat16 [4096, 8192], P('col', 'row')
- passage_grad: bfloat16 [4096, 8192], P('row', 'col')
The draws below stay inside these ranges and needn't reach their ends.
All inputs are finite; a program needn't handle non-finite values.
Results may differ from the reference program's by a relative error of at most 0.0044.
Values may be sent and summed in bfloat16 or wider, within the bound.
A program may use at most 64 MiB of HBM per device.

```python
import math
import jax
import jax.numpy as jnp
from jax import lax

D = 4096
QB = 512
NQ = 8192
NP = 8192


def drawn_embeddings(key, salt, columns):
    normal_draw = jax.random.truncated_normal(jax.random.fold_in(key, salt), -4.0, 4.0, (D, columns), jnp.float32)
    return normal_draw * (2.0 / math.sqrt(D))


def draw_queries(key, part):
    values = drawn_embeddings(key, 11, NQ)
    return jnp.clip(values, -1.0, 1.0).astype(jnp.bfloat16)


def draw_passages(key, part):
    values = drawn_embeddings(key, 12, NP)
    return jnp.clip(values, -1.0, 1.0).astype(jnp.bfloat16)


def teacher_base(key, salt):
    return 4.0 * jax.random.truncated_normal(jax.random.fold_in(key, salt), -4.0, 4.0, (NQ, NP), jnp.float32)


def draw_ce_scores(key, part):
    logits = teacher_base(key, 31)
    return logits


def draw_colbert_scores(key, part):
    logits = teacher_base(key, 32)
    return logits


def place_ends(values, own_key, least, largest):
    spot = [jax.random.randint(jax.random.fold_in(own_key, axis), (), 0, length) for axis, length in enumerate(values.shape)]
    longest = values.shape.index(max(values.shape))
    beside = spot[:longest] + [(spot[longest] + 1) % values.shape[longest]] + spot[longest + 1:]
    return values.at[tuple(spot)].set(least).at[tuple(beside)].set(largest)


def setup_inputs(seed: int = 0) -> dict:
    key_list = jax.random.split(jax.random.key(seed), 7)
    queries = draw_queries(jax.random.fold_in(key_list[6], 71), 0)
    passages = draw_passages(jax.random.fold_in(key_list[6], 71), 0)
    ce_scores = draw_ce_scores(jax.random.fold_in(key_list[6], 71), 0)
    colbert_scores = draw_colbert_scores(jax.random.fold_in(key_list[6], 71), 0)
    mix = place_ends(jax.random.randint(key_list[4], (NQ,), 1, 256), jax.random.fold_in(key_list[4], 1), 1, 255).astype(jnp.int32)
    positive = place_ends(jax.random.randint(key_list[5], (NQ,), 0, NP), jax.random.fold_in(key_list[5], 1), 0, NP - 1).astype(jnp.int32)
    return dict(queries=queries, passages=passages, ce_scores=ce_scores, colbert_scores=colbert_scores, mix=mix, positive=positive)


def reference(queries, passages, ce_scores, colbert_scores, mix, positive):
    count = NQ // QB

    def step(carry, index):
        start = (index * QB).astype(jnp.int32)
        query_block = lax.dynamic_slice_in_dim(queries, start, QB, 1)
        ce_block = lax.dynamic_slice_in_dim(ce_scores, start, QB, 0).astype(jnp.float32)
        col_block = lax.dynamic_slice_in_dim(colbert_scores, start, QB, 0).astype(jnp.float32)
        share = lax.dynamic_slice_in_dim(mix, start, QB, 0).astype(jnp.float32) / 256.0
        target = lax.dynamic_slice_in_dim(positive, start, QB, 0)
        scores = jnp.dot(query_block.T, passages, preferred_element_type=jnp.float32) / 0.05
        teacher = share[:, None] * ce_block + (1.0 - share[:, None]) * col_block
        student_prob = jax.nn.softmax(scores, axis=1)
        teacher_prob = jax.nn.softmax(teacher, axis=1)
        columns = jnp.arange(NP, dtype=jnp.int32)
        onehot = (columns[None, :] == target[:, None]).astype(jnp.float32)
        grad_scores = ((1.5 * student_prob - teacher_prob - 0.5 * onehot) / 0.05).astype(jnp.bfloat16)
        block_grad = jnp.dot(passages, grad_scores.T, preferred_element_type=jnp.float32).astype(jnp.bfloat16)
        carry = carry + jnp.dot(query_block, grad_scores, preferred_element_type=jnp.float32)
        return carry, block_grad

    start_sum = jnp.zeros((D, NP), jnp.float32)
    total, blocks = lax.scan(step, start_sum, jnp.arange(count, dtype=jnp.int32))
    query_grad = jnp.transpose(blocks, (1, 0, 2)).reshape(D, NQ)
    return query_grad, total.astype(jnp.bfloat16)
```

```python
import functools

import jax
import jax.numpy as jnp
from jax import lax
from jax.experimental import pallas as pl
from jax.experimental.pallas import tpu as pltpu
from jax.sharding import PartitionSpec as P

MESH = pl.DeviceIdType.MESH
DELTA = ((1, 0), (0, 1), (-1, 0), (0, -1))
LAG = 3
PIECES = 4


def far(offset):
    return sum(min(o, 4 - o) for o in offset)


def tree_edges(piece):
    base = [((0, 0), 0), ((1, 0), 0), ((0, 0), 2)]
    for x in range(4):
        base += [((x, 0), 1), ((x, 1), 1), ((x, 0), 3)]
    edges = []
    for (x, y), direction in base:
        for _ in range(piece):
            x, y = -y, x
        direction = (direction + piece) % 4
        dx, dy = DELTA[direction]
        edges.append(((x % 4, y % 4), direction, ((x + dx) % 4, (y + dy) % 4)))
    return edges


def xy_schedule():
    trees = [tree_edges(piece) for piece in range(PIECES)]

    def weight(piece, node):
        below = [weight(piece, to) for start, _, to in trees[piece] if start == node]
        return (1 + max(b[0] for b in below), 1 + sum(b[1] for b in below)) if below else (0, 1)

    ready = {(piece, (0, 0)): 0 for piece in range(PIECES)}
    left = {(piece,) + edge for piece in range(PIECES) for edge in trees[piece]}
    plan = [[] for _ in range(4)]
    slot = 0
    while left:
        taken = []
        for direction in range(4):
            able = [e for e in left if e[2] == direction and ready.get((e[0], e[1]), 99) <= slot]
            if able:
                able.sort(key=lambda e: (-far(e[3]), weight(e[0], e[3]), -((e[0] - direction) % 4)), reverse=True)
                taken.append(able[0])
        for piece, start, direction, to in taken:
            left.remove((piece, start, direction, to))
            plan[direction].append((piece, start, to))
            ready[piece, to] = slot + LAG
        slot += 1
    return plan


GATHER_XY = xy_schedule()
REDUCE_XY = [[(p, to, start) for p, start, to in reversed(GATHER_XY[(d + 2) % 4])] for d in range(4)]
HALVES = ((0, 1, 2, 3), (2, 3, 0, 1))
GATHER_Z = [
    [(k, u, False) for k in range(3) for u in h] + [(3, h[0], False), (3, h[1], False), (3, h[1], True)]
    for h in HALVES
]
REDUCE_Z = [
    [(4, h[1], False), (4, h[1], True), (4, h[0], False)]
    + [(k, u, False) for k in (3, 2, 1) for u in (h[2], h[3], h[1], h[0])]
    for h in HALVES
]
FAR_PAIR = [h[0] for h in HALVES]
SLOTS_XY = len(GATHER_XY[0])
SLOTS_Z = len(GATHER_Z[0])
OFFSETS = [(x, y) for x in range(4) for y in range(4)]


def pick(index, values):
    out = jnp.int32(values[0])
    for at, value in enumerate(values[1:], 1):
        out = jnp.where(index == at, jnp.int32(value), out)
    return out


def kernel(
    q_hbm, p_hbm, ce_hbm, cb_hbm, mix_hbm, pos_hbm,
    out_ref,
    q_all, p_all, ce_v, cb_v, mix_ref, pos_ref, s_acc, t_acc, gs_t, st_s, st_t,
    pg_acc, qg_acc, pair_out, pair_in, xy_out, xy_in, z_out, z_in,
    local_sem, send_sem, gxy_sem, gz_sem, gpair_sem, st_sem, rxy_sem, rz_sem, rpair_sem,
):
    row, col = lax.axis_index("row"), lax.axis_index("col")
    x, y, z, core = row // 4, row % 4, col // 2, col % 2
    depth, width = q_hbm.shape
    unit = depth // PIECES

    def row_at(dx, dy):
        return ((x + dx + 4) % 4) * 4 + (y + dy + 4) % 4

    def z_at(dz):
        return (z + dz + 8) % 8

    xy_dev = [(row_at(dx, dy), col) for dx, dy in DELTA]
    z_dev = [(row, z_at(1) * 2 + core), (row, z_at(-1) * 2 + core)]
    cross_dev = [(row, z_at(1) * 2 + 1 - core), (row, z_at(-1) * 2 + 1 - core)]
    pair_dev = (row, z * 2 + 1 - core)

    def shard(ref, index):
        return ref.at[pl.ds(pl.multiple_of(index * depth, depth), depth)]

    def piece(ref, index, u):
        return ref.at[pl.ds(pl.multiple_of(index * depth + u * unit, unit), unit)]

    def remote(src, dst, ssem, rsem, dev):
        return pltpu.make_async_remote_copy(
            src_ref=src, dst_ref=dst, send_sem=ssem, recv_sem=rsem, device_id=dev, device_id_type=MESH
        )

    barrier = pltpu.get_barrier_semaphore()
    for dev in xy_dev + z_dev + [pair_dev]:
        pl.semaphore_signal(barrier, inc=1, device_id=dev, device_id_type=MESH)
    loads = [
        pltpu.make_async_copy(src, dst, local_sem.at[at])
        for at, (src, dst) in enumerate(
            (
                (q_hbm, shard(q_all, col)),
                (p_hbm, shard(p_all, row)),
                (ce_hbm, ce_v),
                (cb_hbm, cb_v),
                (mix_hbm, mix_ref),
                (pos_hbm, pos_ref),
            )
        )
    ]
    for load in loads:
        load.start()
    pl.semaphore_wait(barrier, 7)

    def row_from(off):
        return row_at(-off[0], -off[1])

    def gxy_copy(d, t):
        p, start, _ = GATHER_XY[d][t]
        ref = piece(p_all, row_from(start), p)
        src = p_hbm.at[pl.ds(p * unit, unit)] if start == (0, 0) else ref
        return remote(src, ref, send_sem.at[d], gxy_sem.at[d * SLOTS_XY + t], xy_dev[d])

    def gxy_wait(d, t):
        p, _, to = GATHER_XY[d][t]
        ref = piece(p_all, row_from(to), p)
        remote(ref, ref, send_sem.at[d], gxy_sem.at[d * SLOTS_XY + t], xy_dev[d]).wait_recv()

    def z_from(d, k, core_of):
        return z_at(-k if d == 0 else k) * 2 + core_of

    def gz_copy(d, t):
        k, u, cross = GATHER_Z[d][t]
        ref = piece(q_all, z_from(d, k, core), u)
        src = q_hbm.at[pl.ds(u * unit, unit)] if k == 0 else ref
        dev = cross_dev[d] if cross else z_dev[d]
        return remote(src, ref, send_sem.at[4 + d], gz_sem.at[d * SLOTS_Z + t], dev)

    def gz_wait(d, t):
        k, u, cross = GATHER_Z[d][t]
        ref = piece(q_all, z_from(d, k + 1, 1 - core if cross else core), u)
        dev = cross_dev[d] if cross else z_dev[d]
        remote(ref, ref, send_sem.at[4 + d], gz_sem.at[d * SLOTS_Z + t], dev).wait_recv()
        offset = (k + 1) if d == 1 else (8 - k - 1)
        if k < 3:
            remote(ref, ref, send_sem.at[6], gpair_sem.at[offset], pair_dev).start()
        elif u == FAR_PAIR[d]:
            remote(ref, ref, send_sem.at[6], gpair_sem.at[8 * d], pair_dev).start()

    def gpair_wait(offset):
        other = z_at(offset) * 2 + 1 - core
        if offset == 4:
            for d in range(2):
                ref = piece(q_all, other, FAR_PAIR[d])
                remote(ref, ref, send_sem.at[6], gpair_sem.at[8 * d], pair_dev).wait_recv()
        else:
            ref = shard(q_all, other)
            at = 4 if offset == 0 else offset
            remote(ref, ref, send_sem.at[6], gpair_sem.at[at], pair_dev).wait_recv()

    last_step = SLOTS_XY + LAG - 1
    p_steps = [0] * 5
    for d in range(4):
        for t, (_, _, to) in enumerate(GATHER_XY[d]):
            p_steps[far(to)] = max(p_steps[far(to)], t + LAG)
    z_steps = [0] * 5
    for d in range(2):
        for t, (k, _, cross) in enumerate(GATHER_Z[d]):
            z_steps[k + 1] = max(z_steps[k + 1], t + LAG - (1 if cross else 0))

    s_acc[...] = jnp.zeros_like(s_acc)

    def add_scores(lo, hi):
        def body(i, carry):
            dx, dy, dz = jnp.abs(x - i // 4), jnp.abs(y - i % 4), jnp.abs(z - i // 2)
            p_far = jnp.minimum(dx, 4 - dx) + jnp.minimum(dy, 4 - dy)
            z_far = jnp.minimum(dz, 8 - dz)
            other = jnp.where(i % 2 == core, 0, 1)
            at = jnp.maximum(pick(p_far, p_steps), pick(z_far, z_steps) + other)

            @pl.when(jnp.logical_and(at >= lo, at <= hi))
            def _():
                start = pl.multiple_of(i * depth, depth)
                s_acc[...] += lax.dot_general(
                    p_all[pl.ds(start, depth), :],
                    q_all[pl.ds(start, depth), :],
                    (((0,), (0,)), ((), ())),
                    preferred_element_type=jnp.float32,
                )

            return carry

        lax.fori_loop(0, 16, body, 0)

    def teacher():
        for load in loads:
            load.wait()
        share = mix_ref[...].astype(jnp.float32) / 256.0
        top = jnp.full((1, width), -jnp.inf, jnp.float32)
        for b in range(width // 128):
            lanes = pl.ds(b * 128, 128)
            t = share * ce_v[:, lanes].T + (1.0 - share) * cb_v[:, lanes].T
            t_acc[lanes, :] = t
            top = jnp.maximum(top, jnp.max(t, axis=0, keepdims=True))
        return top

    rows_at_once = 32
    blocks = width // rows_at_once

    def exp_sum(ref, top, scale):
        def body(b, total):
            rows = pl.ds(pl.multiple_of(b * rows_at_once, rows_at_once), rows_at_once)
            e = jnp.exp((ref[rows, :] - top) * scale)
            ref[rows, :] = e
            return total + jnp.sum(e.reshape(rows_at_once // 8, 8, width), axis=0)

        total = lax.fori_loop(0, blocks, body, jnp.zeros((8, width), jnp.float32))
        return jnp.sum(total, axis=0, keepdims=True)

    def put_stats(ref, top, total):
        for k in range(width // 128):
            ref[col, pl.ds(k, 1), :] = top[:, k * 128:(k + 1) * 128]
            ref[col, pl.ds(4 + k, 1), :] = total[:, k * 128:(k + 1) * 128]

    def send_stats(ref, which):
        def body(j, carry):
            k = 8 + ((j + 1) // 2) * (1 - 2 * (j % 2))
            to = (col + k) % 16
            remote(
                ref.at[col], ref.at[col], send_sem.at[7 + which], st_sem.at[which * 16 + k], (row, to)
            ).start()
            return carry

        lax.fori_loop(0, 15, body, 0)

    def wait_stats(ref, which):
        def body(k, carry):
            src = (col - k + 16) % 16
            remote(
                ref.at[src], ref.at[src], send_sem.at[7 + which], st_sem.at[which * 16 + k], (row, src)
            ).wait_recv()
            return carry

        lax.fori_loop(1, 16, body, 0)

    def combine(ref, scale):
        everyone = ref[...]
        tops, totals = everyone[:, 0:4, :], everyone[:, 4:8, :]
        top = jnp.max(tops, axis=0)
        total = jnp.sum(totals * jnp.exp((tops - top[None]) * scale), axis=0)
        mine = ref[col]
        return jnp.exp((mine[0:4, :] - top) * scale) / total

    computed = 0
    for t in range(last_step + 1):
        for d in range(4):
            if 0 <= t - LAG < SLOTS_XY:
                gxy_wait(d, t - LAG)
        for d in range(2):
            if 0 <= t - LAG < SLOTS_Z:
                gz_wait(d, t - LAG)
        for d in range(2):
            if t < SLOTS_Z:
                gz_copy(d, t).start()
        for d in range(4):
            if t < SLOTS_XY:
                gxy_copy(d, t).start()
        if t == 0:
            remote(q_hbm, shard(q_all, col), send_sem.at[6], gpair_sem.at[4], pair_dev).start()
        if t == LAG:
            gpair_wait(0)
        for offset in range(1, 8):
            if z_steps[min(offset, 8 - offset)] + 1 == t:
                gpair_wait(offset)
        if t == 2:
            t_top = teacher()
            t_total = exp_sum(t_acc, t_top, 1.0)
            put_stats(st_t, t_top, t_total)
        if t == last_step:
            send_stats(st_t, 1)
        if t in (7, 10, 11, 12, 14, 15, 16, last_step):
            add_scores(computed, t)
            computed = t + 1

    def max_body(b, top):
        rows = pl.ds(pl.multiple_of(b * rows_at_once, rows_at_once), rows_at_once)
        return jnp.maximum(top, jnp.max(s_acc[rows, :].reshape(rows_at_once // 8, 8, width), axis=0))

    s_top = lax.fori_loop(0, blocks, max_body, jnp.full((8, width), -jnp.inf, jnp.float32))
    s_top = jnp.max(s_top, axis=0, keepdims=True)
    s_total = exp_sum(s_acc, s_top, 20.0)
    put_stats(st_s, s_top, s_total)
    send_stats(st_s, 0)

    wait_stats(st_t, 1)
    t_scale = combine(st_t, 1.0) * -20.0
    target = pos_ref[...] - col * width

    def teacher_body(b, carry):
        start = pl.multiple_of(b * rows_at_once, rows_at_once)
        rows = pl.ds(start, rows_at_once)
        scale = jnp.concatenate([t_scale[k:k + 1, :] for k in range(4)], axis=1)
        index = lax.broadcasted_iota(jnp.int32, (rows_at_once, width), 0) + start
        t_acc[rows, :] = t_acc[rows, :] * scale - jnp.where(index == target, 10.0, 0.0)
        return carry

    lax.fori_loop(0, blocks, teacher_body, 0)

    wait_stats(st_s, 0)
    s_scale = combine(st_s, 20.0) * 30.0

    def grad_body(b, carry):
        rows = pl.ds(pl.multiple_of(b * rows_at_once, rows_at_once), rows_at_once)
        scale = jnp.concatenate([s_scale[k:k + 1, :] for k in range(4)], axis=1)
        gs_t[rows, :] = (s_acc[rows, :] * scale + t_acc[rows, :]).astype(jnp.bfloat16)
        return carry

    lax.fori_loop(0, blocks, grad_body, 0)

    def query_part(offset, core_of):
        lhs = shard(p_all, z_at(offset) * 2 + core_of)[...]
        return jnp.dot(lhs, gs_t[...], preferred_element_type=jnp.float32)

    def pair_copies(offset):
        if offset != 4:
            whole = pair_out.at[offset], pair_in.at[offset]
            return [remote(*whole, send_sem.at[15], rpair_sem.at[offset], pair_dev)]
        return [
            remote(
                pair_out.at[4, pl.ds(u * unit, unit)], pair_in.at[4, pl.ds(u * unit, unit)],
                send_sem.at[15], rpair_sem.at[4 + 4 * at], pair_dev,
            )
            for at, u in enumerate(FAR_PAIR)
        ]

    def query_pair(offset):
        pair_out[offset] = query_part(offset, 1 - core).astype(jnp.bfloat16)
        for copy in pair_copies(offset):
            copy.start()

    def query_own(offset):
        qg_acc[offset] = query_part(offset, core)
        if offset != 4:
            pair_copies(offset)[0].wait_recv()

    passage_done = set()

    def passage_part(off):
        if off not in passage_done:
            passage_done.add(off)
            lhs = shard(q_all, row_from(off))[...]
            pg_acc[OFFSETS.index(off)] = lax.dot_general(
                lhs, gs_t[...], (((1,), (1,)), ((), ())), preferred_element_type=jnp.float32
            )

    def rxy_copy(d, t):
        return remote(
            xy_out.at[d * SLOTS_XY + t], xy_in.at[d * SLOTS_XY + t], send_sem.at[9 + d],
            rxy_sem.at[d * SLOTS_XY + t], xy_dev[d],
        )

    def xy_sum(p, off):
        total = pg_acc[OFFSETS.index(off), pl.ds(p * unit, unit), :]
        for d in range(4):
            for t, (p2, _, to) in enumerate(REDUCE_XY[d]):
                if p2 == p and to == off:
                    rxy_copy(d, t).wait_recv()
                    total += xy_in[d * SLOTS_XY + t].astype(jnp.float32)
        return total

    def rz_copy(d, t):
        _, u, cross = REDUCE_Z[d][t]
        src = pair_out.at[4, pl.ds(u * unit, unit)] if cross else z_out.at[d * SLOTS_Z + t]
        dev = cross_dev[d] if cross else z_dev[d]
        return remote(src, z_in.at[d * SLOTS_Z + t], send_sem.at[13 + d], rz_sem.at[d * SLOTS_Z + t], dev)

    def z_sum(directions, k, u):
        offset = (k if directions[0] == 0 else 8 - k) % 8
        rows = pl.ds(u * unit, unit)
        total = qg_acc[offset, rows, :]
        if k < 4:
            total += pair_in[offset, rows, :].astype(jnp.float32)
        elif u == FAR_PAIR[directions[0]]:
            pair_copies(4)[directions[0]].wait_recv()
            total += pair_in[offset, rows, :].astype(jnp.float32)
        for d in directions:
            for t, (k2, u2, _) in enumerate(REDUCE_Z[d]):
                if (k2, u2) == (k + 1, u):
                    rz_copy(d, t).wait_recv()
                    total += z_in[d * SLOTS_Z + t].astype(jnp.float32)
        return total

    query_pair(4)
    passage_part((2, 2))
    query_own(4)
    for t in range(SLOTS_XY):
        for d in range(4):
            p, off, _ = REDUCE_XY[d][t]
            passage_part(off)
            xy_out[d * SLOTS_XY + t] = xy_sum(p, off).astype(jnp.bfloat16)
            rxy_copy(d, t).start()
        for d in range(2):
            k, u, cross = REDUCE_Z[d][t]
            if not cross:
                z_out[d * SLOTS_Z + t] = z_sum((d,), k, u).astype(jnp.bfloat16)
            rz_copy(d, t).start()
        for at, offset in ((0, 3), (0, 5), (3, 2), (3, 6), (7, 1), (7, 7), (10, 0)):
            if t == at:
                query_pair(offset)
            if t == at + 1:
                query_own(offset)
    passage_part((0, 0))
    for u in range(PIECES):
        rows = pl.ds(u * unit, unit)
        out_ref[pl.ds(depth + u * unit, unit), :] = xy_sum(u, (0, 0)).astype(jnp.bfloat16)
        out_ref[rows, :] = z_sum((0, 1), 0, u).astype(jnp.bfloat16)

    def sent(ref, sem, dev):
        remote(ref, ref, sem, sem, dev).wait_send()

    for d in range(4):
        sent(p_all.at[pl.ds(0, SLOTS_XY * unit)], send_sem.at[d], xy_dev[d])
        sent(xy_out.at[pl.ds(d * SLOTS_XY, SLOTS_XY)], send_sem.at[9 + d], xy_dev[d])
    for d in range(2):
        sent(q_all.at[pl.ds(0, SLOTS_Z * unit)], send_sem.at[4 + d], z_dev[d])
        sent(z_out.at[pl.ds(d * SLOTS_Z, SLOTS_Z)], send_sem.at[13 + d], z_dev[d])
    sent(q_all.at[pl.ds(0, 30 * unit)], send_sem.at[6], pair_dev)
    sent(q_all.at[pl.ds(0, 30 * unit)], send_sem.at[15], pair_dev)
    sent(st_s.at[pl.ds(0, 15)], send_sem.at[7], pair_dev)
    sent(st_t.at[pl.ds(0, 15)], send_sem.at[8], pair_dev)


def per_device(queries, passages, ce_scores, colbert_scores, mix, positive):
    depth, width = queries.shape
    unit = depth // PIECES
    bf16, f32 = jnp.bfloat16, jnp.float32
    hbm = pl.BlockSpec(memory_space=pl.ANY)
    vmem = pl.BlockSpec(memory_space=pltpu.VMEM)
    out = pltpu.VMEM((2 * depth, width), bf16)
    dma = pltpu.SemaphoreType.DMA
    grads = pl.pallas_call(
        kernel,
        out_shape=out,
        in_specs=[hbm] * 6,
        out_specs=vmem,
        scratch_shapes=[
            pltpu.VMEM((16 * depth, width), bf16),
            pltpu.VMEM((16 * depth, width), bf16),
            pltpu.VMEM((width, width), f32),
            pltpu.VMEM((width, width), f32),
            pltpu.VMEM((1, width), jnp.int32),
            pltpu.VMEM((1, width), jnp.int32),
            pltpu.VMEM((width, width), f32),
            pltpu.VMEM((width, width), f32),
            pltpu.VMEM((width, width), bf16),
            pltpu.VMEM((16, 8, 128), f32),
            pltpu.VMEM((16, 8, 128), f32),
            pltpu.VMEM((16, depth, width), f32),
            pltpu.VMEM((8, depth, width), f32),
            pltpu.VMEM((8, depth, width), bf16),
            pltpu.VMEM((8, depth, width), bf16),
            pltpu.VMEM((4 * SLOTS_XY, unit, width), bf16),
            pltpu.VMEM((4 * SLOTS_XY, unit, width), bf16),
            pltpu.VMEM((2 * SLOTS_Z, unit, width), bf16),
            pltpu.VMEM((2 * SLOTS_Z, unit, width), bf16),
            dma((6,)),
            dma((16,)),
            dma((4 * SLOTS_XY,)),
            dma((2 * SLOTS_Z,)),
            dma((9,)),
            dma((32,)),
            dma((4 * SLOTS_XY,)),
            dma((2 * SLOTS_Z,)),
            dma((9,)),
        ],
        compiler_params=pltpu.CompilerParams(collective_id=0, has_side_effects=True),
    )(queries, passages, ce_scores, colbert_scores, mix.reshape(1, width), positive.reshape(1, width))
    return grads[:depth], grads[depth:]


def solution(mesh):
    in_specs = (
        P("col", "row"),
        P("row", "col"),
        P("row", "col"),
        P("row", "col"),
        P("row"),
        P("row"),
    )
    out_specs = (P("col", "row"), P("row", "col"))
    return jax.shard_map(
        per_device, mesh=mesh, in_specs=in_specs, out_specs=out_specs, check_vma=False
    )
```

```python
import functools

import jax
import jax.numpy as jnp
from jax import lax
from jax.experimental import pallas as pl
from jax.experimental.pallas import tpu as pltpu
from jax.sharding import PartitionSpec as P

MESH = pl.DeviceIdType.MESH
DELTA = ((1, 0), (0, 1), (-1, 0), (0, -1))
LAG = 4
PIECES = 4


def far(offset):
    return sum(min(o, 4 - o) for o in offset)


def group(offset):
    two_x, two_y = offset[0] == 2, offset[1] == 2
    if far(offset) == 3:
        return 5 if two_x else 3
    return 6 if far(offset) == 2 and (two_x or two_y) else far(offset)


TURNS = {(2, 0): 0, (0, 2): 0, (1, 1): 1, (3, 3): 1, (3, 1): 2, (1, 3): 2, (1, 2): 0, (3, 2): 0, (2, 1): 1, (2, 3): 1}


def tree_edges(piece):
    base = [((0, 0), 0), ((1, 0), 0), ((0, 0), 2)]
    for x in range(4):
        base += [((x, 0), 1), ((x, 1), 1), ((x, 0), 3)]
    edges = []
    for (x, y), direction in base:
        for _ in range(piece):
            x, y = -y, x
        direction = (direction + piece) % 4
        dx, dy = DELTA[direction]
        edges.append(((x % 4, y % 4), direction, ((x + dx) % 4, (y + dy) % 4)))
    return edges


def xy_schedule():
    trees = [tree_edges(piece) for piece in range(PIECES)]

    def late(piece, node):
        return far(node) == 3 and all(start != node for start, _, _ in trees[piece])

    ready = {(piece, (0, 0)): 0 for piece in range(PIECES)}
    left = {(piece,) + edge for piece in range(PIECES) for edge in trees[piece]}
    plan = [[] for _ in range(4)]
    slot = 0
    while left:
        taken = []
        for direction in range(4):
            able = [e for e in left if e[2] == direction and ready.get((e[0], e[1]), 99) <= slot]
            if able:
                able.sort(key=lambda e: (far(e[3]), late(e[0], e[3]), TURNS.get(e[3], (0, 2, 3, 1)[(e[0] - direction) % 4])))
                taken.append(able[0])
        for piece, start, direction, to in taken:
            left.remove((piece, start, direction, to))
            plan[direction].append((piece, start, to))
            ready[piece, to] = slot + LAG
        slot += 1
    return plan


GATHER_XY = xy_schedule()
REDUCE_XY = [[(p, to, start) for p, start, to in reversed(GATHER_XY[(d + 2) % 4])] for d in range(4)]
HALVES = ((0, 1, 2, 3), (2, 3, 0, 1))
GATHER_Z = [
    [(k, u, False) for k in range(3) for u in h] + [(3, h[0], False), (3, h[1], False), (3, h[1], True)]
    for h in HALVES
]
REDUCE_Z = [
    [(4, h[1], False), (4, h[1], True), (4, h[0], False)]
    + [(k, u, False) for k in (3, 2, 1) for u in (h[2], h[3], h[1], h[0])]
    for h in HALVES
]
FAR_PAIR = [h[0] for h in HALVES]
SLOTS_XY = len(GATHER_XY[0])
SLOTS_Z = len(GATHER_Z[0])
OFFSETS = [(x, y) for x in range(4) for y in range(4)]


def pick(index, values):
    out = jnp.int32(values[0])
    for at, value in enumerate(values[1:], 1):
        out = jnp.where(index == at, jnp.int32(value), out)
    return out


def kernel(
    q_hbm, p_hbm, ce_hbm, cb_hbm, mix_hbm, pos_hbm,
    out_ref,
    q_all, p_all, ce_v, cb_v, mix_ref, pos_ref, s_acc, t_acc, gs_t, st_s, st_t,
    pg_acc, qg_acc, pair_out, pair_in, xy_out, xy_in, z_out, z_in,
    local_sem, send_sem, gxy_sem, gz_sem, gpair_sem, st_sem, rxy_sem, rz_sem, rpair_sem,
):
    row, col = lax.axis_index("row"), lax.axis_index("col")
    x, y, z, core = row // 4, row % 4, col // 2, col % 2
    depth, width = q_hbm.shape
    unit = depth // PIECES

    def row_at(dx, dy):
        return ((x + dx + 4) % 4) * 4 + (y + dy + 4) % 4

    def z_at(dz):
        return (z + dz + 8) % 8

    xy_dev = [(row_at(dx, dy), col) for dx, dy in DELTA]
    z_dev = [(row, z_at(1) * 2 + core), (row, z_at(-1) * 2 + core)]
    cross_dev = [(row, z_at(1) * 2 + 1 - core), (row, z_at(-1) * 2 + 1 - core)]
    pair_dev = (row, z * 2 + 1 - core)

    def shard(ref, index):
        return ref.at[pl.ds(pl.multiple_of(index * depth, depth), depth)]

    def piece(ref, index, u):
        return ref.at[pl.ds(pl.multiple_of(index * depth + u * unit, unit), unit)]

    def remote(src, dst, ssem, rsem, dev):
        return pltpu.make_async_remote_copy(
            src_ref=src, dst_ref=dst, send_sem=ssem, recv_sem=rsem, device_id=dev, device_id_type=MESH
        )

    barrier = pltpu.get_barrier_semaphore()
    for dev in xy_dev + z_dev + [pair_dev]:
        pl.semaphore_signal(barrier, inc=1, device_id=dev, device_id_type=MESH)
    loads = [
        pltpu.make_async_copy(src, dst, local_sem.at[at])
        for at, (src, dst) in enumerate(
            (
                (q_hbm, shard(q_all, col)),
                (p_hbm, shard(p_all, row)),
                (ce_hbm, ce_v),
                (cb_hbm, cb_v),
                (mix_hbm, mix_ref),
                (pos_hbm, pos_ref),
            )
        )
    ]
    for load in loads:
        load.start()
    pl.semaphore_wait(barrier, 7)

    def row_from(off):
        return row_at(-off[0], -off[1])

    def gxy_copy(d, t):
        p, start, _ = GATHER_XY[d][t]
        ref = piece(p_all, row_from(start), p)
        src = p_hbm.at[pl.ds(p * unit, unit)] if start == (0, 0) else ref
        return remote(src, ref, send_sem.at[d], gxy_sem.at[d * SLOTS_XY + t], xy_dev[d])

    def gxy_wait(d, t):
        p, _, to = GATHER_XY[d][t]
        ref = piece(p_all, row_from(to), p)
        remote(ref, ref, send_sem.at[d], gxy_sem.at[d * SLOTS_XY + t], xy_dev[d]).wait_recv()

    def z_from(d, k, core_of):
        return z_at(-k if d == 0 else k) * 2 + core_of

    def gz_copy(d, t):
        k, u, cross = GATHER_Z[d][t]
        ref = piece(q_all, z_from(d, k, core), u)
        src = q_hbm.at[pl.ds(u * unit, unit)] if k == 0 else ref
        dev = cross_dev[d] if cross else z_dev[d]
        return remote(src, ref, send_sem.at[4 + d], gz_sem.at[d * SLOTS_Z + t], dev)

    def gz_wait(d, t):
        k, u, cross = GATHER_Z[d][t]
        ref = piece(q_all, z_from(d, k + 1, 1 - core if cross else core), u)
        dev = cross_dev[d] if cross else z_dev[d]
        remote(ref, ref, send_sem.at[4 + d], gz_sem.at[d * SLOTS_Z + t], dev).wait_recv()
        offset = (k + 1) if d == 1 else (8 - k - 1)
        if k < 3:
            remote(ref, ref, send_sem.at[6], gpair_sem.at[offset], pair_dev).start()
        elif u == FAR_PAIR[d]:
            remote(ref, ref, send_sem.at[6], gpair_sem.at[8 * d], pair_dev).start()

    def gpair_wait(offset):
        other = z_at(offset) * 2 + 1 - core
        if offset == 4:
            for d in range(2):
                ref = piece(q_all, other, FAR_PAIR[d])
                remote(ref, ref, send_sem.at[6], gpair_sem.at[8 * d], pair_dev).wait_recv()
        else:
            ref = shard(q_all, other)
            at = 4 if offset == 0 else offset
            remote(ref, ref, send_sem.at[6], gpair_sem.at[at], pair_dev).wait_recv()

    last_step = SLOTS_XY + LAG - 1
    p_steps = [0] * 7
    for d in range(4):
        for t, (_, _, to) in enumerate(GATHER_XY[d]):
            p_steps[group(to)] = max(p_steps[group(to)], t + LAG)
    z_steps = [0] * 5
    for d in range(2):
        for t, (k, _, cross) in enumerate(GATHER_Z[d]):
            z_steps[k + 1] = max(z_steps[k + 1], t + LAG - (1 if cross else 0))


    def add_scores(lo, hi):
        def body(i, carry):
            dx, dy, dz = jnp.abs(x - i // 4), jnp.abs(y - i % 4), jnp.abs(z - i // 2)
            dx, dy = jnp.minimum(dx, 4 - dx), jnp.minimum(dy, 4 - dy)
            p_far = dx + dy
            two = jnp.where(p_far == 2, jnp.maximum(dx, dy), 0) == 2
            p_far = jnp.where(two, 6, jnp.where(jnp.where(p_far == 3, dx, 0) == 2, 5, p_far))
            z_far = jnp.minimum(dz, 8 - dz)
            other = jnp.where(i % 2 == core, 0, 1)
            at = jnp.maximum(pick(p_far, p_steps), pick(z_far, z_steps) + other)

            @pl.when(jnp.logical_and(at >= lo, at <= hi))
            def _():
                start = pl.multiple_of(i * depth, depth)
                s_acc[...] += lax.dot_general(
                    p_all[pl.ds(start, depth), :],
                    q_all[pl.ds(start, depth), :],
                    (((0,), (0,)), ((), ())),
                    preferred_element_type=jnp.float32,
                )

            return carry

        lax.fori_loop(0, 16, body, 0)

    def teacher():
        for load in loads:
            load.wait()
        share = mix_ref[...].astype(jnp.float32) / 256.0
        top = jnp.full((1, width), -jnp.inf, jnp.float32)
        for b in range(width // 128):
            lanes = pl.ds(b * 128, 128)
            t = share * ce_v[:, lanes].T + (1.0 - share) * cb_v[:, lanes].T
            t_acc[lanes, :] = t
            top = jnp.maximum(top, jnp.max(t, axis=0, keepdims=True))
        return top

    rows_at_once = 64
    blocks = width // rows_at_once

    def exp_sum(ref, top, scale):
        def body(b, total):
            rows = pl.ds(pl.multiple_of(b * rows_at_once, rows_at_once), rows_at_once)
            e = jnp.exp((ref[rows, :] - top) * scale)
            ref[rows, :] = e
            return total + jnp.sum(e.reshape(rows_at_once // 8, 8, width), axis=0)

        total = lax.fori_loop(0, blocks, body, jnp.zeros((8, width), jnp.float32))
        return jnp.sum(total, axis=0, keepdims=True)

    def put_stats(ref, top, total):
        for k in range(width // 128):
            ref[col, pl.ds(k, 1), :] = top[:, k * 128:(k + 1) * 128]
            ref[col, pl.ds(4 + k, 1), :] = total[:, k * 128:(k + 1) * 128]

    def send_stats(ref, which):
        def body(j, carry):
            k = 8 + ((j + 1) // 2) * (1 - 2 * (j % 2))
            to = (col + k) % 16
            remote(
                ref.at[col], ref.at[col], send_sem.at[7 + which], st_sem.at[which * 16 + k], (row, to)
            ).start()
            return carry

        lax.fori_loop(0, 15, body, 0)

    def wait_stats(ref, which):
        def body(k, carry):
            src = (col - k + 16) % 16
            remote(
                ref.at[src], ref.at[src], send_sem.at[7 + which], st_sem.at[which * 16 + k], (row, src)
            ).wait_recv()
            return carry

        lax.fori_loop(1, 16, body, 0)

    def combine(ref, scale):
        everyone = ref[...]
        tops, totals = everyone[:, 0:4, :], everyone[:, 4:8, :]
        top = jnp.max(tops, axis=0)
        total = jnp.sum(totals * jnp.exp((tops - top[None]) * scale), axis=0)
        mine = ref[col]
        return jnp.exp((mine[0:4, :] - top) * scale) / total

    arrives = {(p, to): (d, t) for d in range(4) for t, (p, _, to) in enumerate(GATHER_XY[d])}
    waited = set()

    def here(wait, d, t):
        if (wait, d, t) not in waited:
            waited.add((wait, d, t))
            wait(d, t)

    computed = 0
    for t in range(last_step + 1):
        for slot in range(4) if t == 0 else (t,) if 4 <= t < SLOTS_XY else ():
            for d in range(2):
                if slot >= 4:
                    here(gz_wait, d, GATHER_Z[d].index((GATHER_Z[d][slot][0] - 1, GATHER_Z[d][slot][1], False)))
                gz_copy(d, slot).start()
            for d in range(4):
                if slot >= 4:
                    here(gxy_wait, *arrives[GATHER_XY[d][slot][:2]])
                gxy_copy(d, slot).start()
        for d in range(2):
            if 0 <= t - LAG < SLOTS_Z:
                here(gz_wait, d, t - LAG)
        for d in range(4):
            if 0 <= t - LAG < SLOTS_XY:
                here(gxy_wait, d, t - LAG)
        if t == 0:
            remote(q_hbm, shard(q_all, col), send_sem.at[6], gpair_sem.at[4], pair_dev).start()
        if t == LAG:
            gpair_wait(0)
        for offset in range(1, 8):
            if z_steps[min(offset, 8 - offset)] + 1 == t:
                gpair_wait(offset)
        if t == 0:
            s_acc[...] = jnp.zeros_like(s_acc)
            t_top = teacher()
            t_total = exp_sum(t_acc, t_top, 1.0)
            put_stats(st_t, t_top, t_total)
        if t == last_step:
            send_stats(st_t, 1)
        if t in (8, 11, 12, 13, 15, 16, 17, last_step):
            add_scores(computed, t)
            computed = t + 1

    def max_body(b, top):
        rows = pl.ds(pl.multiple_of(b * rows_at_once, rows_at_once), rows_at_once)
        return jnp.maximum(top, jnp.max(s_acc[rows, :].reshape(rows_at_once // 8, 8, width), axis=0))

    s_top = lax.fori_loop(0, blocks, max_body, jnp.full((8, width), -jnp.inf, jnp.float32))
    s_top = jnp.max(s_top, axis=0, keepdims=True)
    s_total = exp_sum(s_acc, s_top, 20.0)
    put_stats(st_s, s_top, s_total)
    send_stats(st_s, 0)

    wait_stats(st_t, 1)
    t_scale = combine(st_t, 1.0) * -20.0
    target = pos_ref[...] - col * width

    def teacher_body(b, carry):
        start = pl.multiple_of(b * rows_at_once, rows_at_once)
        rows = pl.ds(start, rows_at_once)
        scale = jnp.concatenate([t_scale[k:k + 1, :] for k in range(4)], axis=1)
        index = lax.broadcasted_iota(jnp.int32, (rows_at_once, width), 0) + start
        t_acc[rows, :] = t_acc[rows, :] * scale - jnp.where(index == target, 10.0, 0.0)
        return carry

    lax.fori_loop(0, blocks, teacher_body, 0)

    wait_stats(st_s, 0)
    s_scale = combine(st_s, 20.0) * 30.0

    def grad_body(b, carry):
        rows = pl.ds(pl.multiple_of(b * rows_at_once, rows_at_once), rows_at_once)
        scale = jnp.concatenate([s_scale[k:k + 1, :] for k in range(4)], axis=1)
        gs_t[rows, :] = (s_acc[rows, :] * scale + t_acc[rows, :]).astype(jnp.bfloat16)
        return carry

    lax.fori_loop(0, blocks, grad_body, 0)

    def query_part(offset, core_of):
        lhs = shard(p_all, z_at(offset) * 2 + core_of)[...]
        return jnp.dot(lhs, gs_t[...], preferred_element_type=jnp.float32)

    def pair_copies(offset):
        if offset != 4:
            whole = pair_out.at[offset], pair_in.at[offset]
            return [remote(*whole, send_sem.at[15], rpair_sem.at[offset], pair_dev)]
        return [
            remote(
                pair_out.at[4, pl.ds(u * unit, unit)], pair_in.at[4, pl.ds(u * unit, unit)],
                send_sem.at[15], rpair_sem.at[4 + 4 * at], pair_dev,
            )
            for at, u in enumerate(FAR_PAIR)
        ]

    def query_pair(offset):
        pair_out[offset] = query_part(offset, 1 - core).astype(jnp.bfloat16)
        for copy in pair_copies(offset):
            copy.start()

    def query_own(offset):
        qg_acc[offset] = query_part(offset, core)

    paired = set()

    passage_done = set()

    def passage_part(off):
        if off not in passage_done:
            passage_done.add(off)
            lhs = shard(q_all, row_from(off))[...]
            pg_acc[OFFSETS.index(off)] = lax.dot_general(
                lhs, gs_t[...], (((1,), (1,)), ((), ())), preferred_element_type=jnp.float32
            )

    def rxy_copy(d, t):
        return remote(
            xy_out.at[d * SLOTS_XY + t], xy_in.at[d * SLOTS_XY + t], send_sem.at[9 + d],
            rxy_sem.at[d * SLOTS_XY + t], xy_dev[d],
        )

    def xy_sum(p, off):
        total = pg_acc[OFFSETS.index(off), pl.ds(p * unit, unit), :]
        for d in range(4):
            for t, (p2, _, to) in enumerate(REDUCE_XY[d]):
                if p2 == p and to == off:
                    rxy_copy(d, t).wait_recv()
                    total += xy_in[d * SLOTS_XY + t].astype(jnp.float32)
        return total

    def rz_copy(d, t):
        _, u, cross = REDUCE_Z[d][t]
        src = pair_out.at[4, pl.ds(u * unit, unit)] if cross else z_out.at[d * SLOTS_Z + t]
        dev = cross_dev[d] if cross else z_dev[d]
        return remote(src, z_in.at[d * SLOTS_Z + t], send_sem.at[13 + d], rz_sem.at[d * SLOTS_Z + t], dev)

    def z_sum(directions, k, u):
        offset = (k if directions[0] == 0 else 8 - k) % 8
        rows = pl.ds(u * unit, unit)
        total = qg_acc[offset, rows, :]
        if k < 4:
            if offset not in paired:
                paired.add(offset)
                pair_copies(offset)[0].wait_recv()
            total += pair_in[offset, rows, :].astype(jnp.float32)
        elif u == FAR_PAIR[directions[0]]:
            pair_copies(4)[directions[0]].wait_recv()
            total += pair_in[offset, rows, :].astype(jnp.float32)
        for d in directions:
            for t, (k2, u2, _) in enumerate(REDUCE_Z[d]):
                if (k2, u2) == (k + 1, u):
                    rz_copy(d, t).wait_recv()
                    total += z_in[d * SLOTS_Z + t].astype(jnp.float32)
        return total

    query_pair(4)
    passage_part((2, 2))
    query_own(4)
    for t in range(SLOTS_XY):
        for d in range(4):
            p, off, _ = REDUCE_XY[d][t]
            passage_part(off)
            xy_out[d * SLOTS_XY + t] = xy_sum(p, off).astype(jnp.bfloat16)
            rxy_copy(d, t).start()
        for d in range(2):
            k, u, cross = REDUCE_Z[d][t]
            if not cross:
                z_out[d * SLOTS_Z + t] = z_sum((d,), k, u).astype(jnp.bfloat16)
            rz_copy(d, t).start()
        for at, offset in ((0, 3), (0, 5), (3, 2), (3, 6), (7, 1), (7, 7), (10, 0)):
            if t == at:
                query_pair(offset)
            if t == at + 1:
                query_own(offset)
    passage_part((0, 0))
    for u in range(PIECES):
        rows = pl.ds(u * unit, unit)
        out_ref[pl.ds(depth + u * unit, unit), :] = xy_sum(u, (0, 0)).astype(jnp.bfloat16)
        out_ref[rows, :] = z_sum((0, 1), 0, u).astype(jnp.bfloat16)

    def sent(ref, sem, dev):
        remote(ref, ref, sem, sem, dev).wait_send()

    for d in range(4):
        sent(p_all.at[pl.ds(0, SLOTS_XY * unit)], send_sem.at[d], xy_dev[d])
        sent(xy_out.at[pl.ds(d * SLOTS_XY, SLOTS_XY)], send_sem.at[9 + d], xy_dev[d])
    for d in range(2):
        sent(q_all.at[pl.ds(0, SLOTS_Z * unit)], send_sem.at[4 + d], z_dev[d])
        sent(z_out.at[pl.ds(d * SLOTS_Z, SLOTS_Z)], send_sem.at[13 + d], z_dev[d])
    sent(q_all.at[pl.ds(0, 30 * unit)], send_sem.at[6], pair_dev)
    sent(q_all.at[pl.ds(0, 30 * unit)], send_sem.at[15], pair_dev)
    sent(st_s.at[pl.ds(0, 15)], send_sem.at[7], pair_dev)
    sent(st_t.at[pl.ds(0, 15)], send_sem.at[8], pair_dev)


def per_device(queries, passages, ce_scores, colbert_scores, mix, positive):
    depth, width = queries.shape
    unit = depth // PIECES
    bf16, f32 = jnp.bfloat16, jnp.float32
    hbm = pl.BlockSpec(memory_space=pl.ANY)
    vmem = pl.BlockSpec(memory_space=pltpu.VMEM)
    out = pltpu.VMEM((2 * depth, width), bf16)
    dma = pltpu.SemaphoreType.DMA
    grads = pl.pallas_call(
        kernel,
        out_shape=out,
        in_specs=[hbm] * 6,
        out_specs=vmem,
        scratch_shapes=[
            pltpu.VMEM((16 * depth, width), bf16),
            pltpu.VMEM((16 * depth, width), bf16),
            pltpu.VMEM((width, width), f32),
            pltpu.VMEM((width, width), f32),
            pltpu.VMEM((1, width), jnp.int32),
            pltpu.VMEM((1, width), jnp.int32),
            pltpu.VMEM((width, width), f32),
            pltpu.VMEM((width, width), f32),
            pltpu.VMEM((width, width), bf16),
            pltpu.VMEM((16, 8, 128), f32),
            pltpu.VMEM((16, 8, 128), f32),
            pltpu.VMEM((16, depth, width), f32),
            pltpu.VMEM((8, depth, width), f32),
            pltpu.VMEM((8, depth, width), bf16),
            pltpu.VMEM((8, depth, width), bf16),
            pltpu.VMEM((4 * SLOTS_XY, unit, width), bf16),
            pltpu.VMEM((4 * SLOTS_XY, unit, width), bf16),
            pltpu.VMEM((2 * SLOTS_Z, unit, width), bf16),
            pltpu.VMEM((2 * SLOTS_Z, unit, width), bf16),
            dma((6,)),
            dma((16,)),
            dma((4 * SLOTS_XY,)),
            dma((2 * SLOTS_Z,)),
            dma((9,)),
            dma((32,)),
            dma((4 * SLOTS_XY,)),
            dma((2 * SLOTS_Z,)),
            dma((9,)),
        ],
        compiler_params=pltpu.CompilerParams(collective_id=0, has_side_effects=True),
    )(queries, passages, ce_scores, colbert_scores, mix.reshape(1, width), positive.reshape(1, width))
    return grads[:depth], grads[depth:]


def solution(mesh):
    in_specs = (
        P("col", "row"),
        P("row", "col"),
        P("row", "col"),
        P("row", "col"),
        P("row"),
        P("row"),
    )
    out_specs = (P("col", "row"), P("row", "col"))
    return jax.shard_map(
        per_device, mesh=mesh, in_specs=in_specs, out_specs=out_specs, check_vma=False
    )
```

```python
import functools

import jax
import jax.numpy as jnp
from jax import lax
from jax.experimental import pallas as pl
from jax.experimental.pallas import tpu as pltpu
from jax.sharding import PartitionSpec as P

MESH = pl.DeviceIdType.MESH
DELTA = ((1, 0), (0, 1), (-1, 0), (0, -1))
LAG = 4
PIECES = 4


def far(offset):
    return sum(min(o, 4 - o) for o in offset)


def group(offset):
    two_x, two_y = offset[0] == 2, offset[1] == 2
    if far(offset) == 3:
        return 5 if two_x else 3
    return 6 if far(offset) == 2 and (two_x or two_y) else far(offset)


TURNS = {(2, 0): 0, (0, 2): 0, (1, 1): 1, (3, 3): 1, (3, 1): 2, (1, 3): 2, (1, 2): 0, (3, 2): 0, (2, 1): 1, (2, 3): 1}


def tree_edges(piece):
    base = [((0, 0), 0), ((1, 0), 0), ((0, 0), 2)]
    for x in range(4):
        base += [((x, 0), 1), ((x, 1), 1), ((x, 0), 3)]
    edges = []
    for (x, y), direction in base:
        for _ in range(piece):
            x, y = -y, x
        direction = (direction + piece) % 4
        dx, dy = DELTA[direction]
        edges.append(((x % 4, y % 4), direction, ((x + dx) % 4, (y + dy) % 4)))
    return edges


def xy_schedule():
    trees = [tree_edges(piece) for piece in range(PIECES)]

    def late(piece, node):
        return far(node) == 3 and all(start != node for start, _, _ in trees[piece])

    ready = {(piece, (0, 0)): 0 for piece in range(PIECES)}
    left = {(piece,) + edge for piece in range(PIECES) for edge in trees[piece]}
    plan = [[] for _ in range(4)]
    slot = 0
    while left:
        taken = []
        for direction in range(4):
            able = [e for e in left if e[2] == direction and ready.get((e[0], e[1]), 99) <= slot]
            if able:
                able.sort(key=lambda e: (far(e[3]), late(e[0], e[3]), TURNS.get(e[3], (0, 2, 3, 1)[(e[0] - direction) % 4])))
                taken.append(able[0])
        for piece, start, direction, to in taken:
            left.remove((piece, start, direction, to))
            plan[direction].append((piece, start, to))
            ready[piece, to] = slot + LAG
        slot += 1
    return plan


GATHER_XY = xy_schedule()
REDUCE_XY = [[(p, to, start) for p, start, to in reversed(GATHER_XY[(d + 2) % 4])] for d in range(4)]
HALVES = ((0, 1, 2, 3), (2, 3, 0, 1))
GATHER_Z = [
    [(k, u, False) for k in range(3) for u in h] + [(3, h[0], False), (3, h[1], False), (3, h[1], True)]
    for h in HALVES
]
REDUCE_Z = [
    [(4, h[1], False), (4, h[1], True), (4, h[0], False)]
    + [(k, u, False) for k in (3, 2, 1) for u in (h[2], h[3], h[1], h[0])]
    for h in HALVES
]
FAR_PAIR = [h[0] for h in HALVES]
SLOTS_XY = len(GATHER_XY[0])
SLOTS_Z = len(GATHER_Z[0])
OFFSETS = [(x, y) for x in range(4) for y in range(4)]


def pick(index, values):
    out = jnp.int32(values[0])
    for at, value in enumerate(values[1:], 1):
        out = jnp.where(index == at, jnp.int32(value), out)
    return out


def kernel(
    q_hbm, p_hbm, ce_hbm, cb_hbm, mix_hbm, pos_hbm,
    out_ref,
    q_all, p_all, ce_v, cb_v, mix_ref, pos_ref, s_acc, t_acc, gs_t, st_s, st_t,
    pg_acc, qg_acc, pair_out, pair_in, xy_out, xy_in, z_out, z_in,
    local_sem, send_sem, gxy_sem, gz_sem, gpair_sem, st_sem, rxy_sem, rz_sem, rpair_sem,
):
    row, col = lax.axis_index("row"), lax.axis_index("col")
    x, y, z, core = row // 4, row % 4, col // 2, col % 2
    depth, width = q_hbm.shape
    unit = depth // PIECES

    def row_at(dx, dy):
        return ((x + dx + 4) % 4) * 4 + (y + dy + 4) % 4

    def z_at(dz):
        return (z + dz + 8) % 8

    xy_dev = [(row_at(dx, dy), col) for dx, dy in DELTA]
    z_dev = [(row, z_at(1) * 2 + core), (row, z_at(-1) * 2 + core)]
    cross_dev = [(row, z_at(1) * 2 + 1 - core), (row, z_at(-1) * 2 + 1 - core)]
    pair_dev = (row, z * 2 + 1 - core)

    def shard(ref, index):
        return ref.at[pl.ds(pl.multiple_of(index * depth, depth), depth)]

    def piece(ref, index, u):
        return ref.at[pl.ds(pl.multiple_of(index * depth + u * unit, unit), unit)]

    def remote(src, dst, ssem, rsem, dev):
        return pltpu.make_async_remote_copy(
            src_ref=src, dst_ref=dst, send_sem=ssem, recv_sem=rsem, device_id=dev, device_id_type=MESH
        )

    barrier = pltpu.get_barrier_semaphore()
    for dev in xy_dev + z_dev + [pair_dev]:
        pl.semaphore_signal(barrier, inc=1, device_id=dev, device_id_type=MESH)
    loads = [
        pltpu.make_async_copy(src, dst, local_sem.at[at])
        for at, (src, dst) in enumerate(
            (
                (q_hbm, shard(q_all, col)),
                (p_hbm, shard(p_all, row)),
                (ce_hbm, ce_v),
                (cb_hbm, cb_v),
                (mix_hbm, mix_ref),
                (pos_hbm, pos_ref),
            )
        )
    ]
    for load in loads:
        load.start()
    pl.semaphore_wait(barrier, 7)

    def row_from(off):
        return row_at(-off[0], -off[1])

    def gxy_copy(d, t):
        p, start, _ = GATHER_XY[d][t]
        ref = piece(p_all, row_from(start), p)
        src = p_hbm.at[pl.ds(p * unit, unit)] if start == (0, 0) else ref
        return remote(src, ref, send_sem.at[d], gxy_sem.at[d * SLOTS_XY + t], xy_dev[d])

    def gxy_wait(d, t):
        p, _, to = GATHER_XY[d][t]
        ref = piece(p_all, row_from(to), p)
        remote(ref, ref, send_sem.at[d], gxy_sem.at[d * SLOTS_XY + t], xy_dev[d]).wait_recv()

    def z_from(d, k, core_of):
        return z_at(-k if d == 0 else k) * 2 + core_of

    def gz_copy(d, t):
        k, u, cross = GATHER_Z[d][t]
        ref = piece(q_all, z_from(d, k, core), u)
        src = q_hbm.at[pl.ds(u * unit, unit)] if k == 0 else ref
        dev = cross_dev[d] if cross else z_dev[d]
        return remote(src, ref, send_sem.at[4 + d], gz_sem.at[d * SLOTS_Z + t], dev)

    def gz_wait(d, t):
        k, u, cross = GATHER_Z[d][t]
        ref = piece(q_all, z_from(d, k + 1, 1 - core if cross else core), u)
        dev = cross_dev[d] if cross else z_dev[d]
        remote(ref, ref, send_sem.at[4 + d], gz_sem.at[d * SLOTS_Z + t], dev).wait_recv()
        offset = (k + 1) if d == 1 else (8 - k - 1)
        if k < 3:
            remote(ref, ref, send_sem.at[6], gpair_sem.at[offset], pair_dev).start()
        elif u == FAR_PAIR[d]:
            remote(ref, ref, send_sem.at[6], gpair_sem.at[8 * d], pair_dev).start()

    def gpair_wait(offset):
        other = z_at(offset) * 2 + 1 - core
        if offset == 4:
            for d in range(2):
                ref = piece(q_all, other, FAR_PAIR[d])
                remote(ref, ref, send_sem.at[6], gpair_sem.at[8 * d], pair_dev).wait_recv()
        else:
            ref = shard(q_all, other)
            at = 4 if offset == 0 else offset
            remote(ref, ref, send_sem.at[6], gpair_sem.at[at], pair_dev).wait_recv()

    last_step = SLOTS_XY + LAG - 1
    p_steps = [0] * 7
    for d in range(4):
        for t, (_, _, to) in enumerate(GATHER_XY[d]):
            p_steps[group(to)] = max(p_steps[group(to)], t + LAG)
    z_steps = [0] * 5
    for d in range(2):
        for t, (k, _, cross) in enumerate(GATHER_Z[d]):
            z_steps[k + 1] = max(z_steps[k + 1], t + LAG - (1 if cross else 0))


    def add_chunk(i):
        start = pl.multiple_of(i * depth, depth)
        s_acc[...] += lax.dot_general(
            p_all[pl.ds(start, depth), :],
            q_all[pl.ds(start, depth), :],
            (((0,), (0,)), ((), ())),
            preferred_element_type=jnp.float32,
        )

    def add_scores(lo, hi):
        def body(i, carry):
            dx, dy, dz = jnp.abs(x - i // 4), jnp.abs(y - i % 4), jnp.abs(z - i // 2)
            dx, dy = jnp.minimum(dx, 4 - dx), jnp.minimum(dy, 4 - dy)
            p_far = dx + dy
            two = jnp.where(p_far == 2, jnp.maximum(dx, dy), 0) == 2
            p_far = jnp.where(two, 6, jnp.where(jnp.where(p_far == 3, dx, 0) == 2, 5, p_far))
            z_far = jnp.minimum(dz, 8 - dz)
            other = jnp.where(i % 2 == core, 0, 1)
            at = jnp.maximum(pick(p_far, p_steps), pick(z_far, z_steps) + other)

            @pl.when(jnp.logical_and(at >= lo, at <= hi))
            def _():
                add_chunk(i)

            return carry

        lax.fori_loop(0, 16, body, 0)

    def teacher():
        for load in loads:
            load.wait()
        share = mix_ref[...].astype(jnp.float32) / 256.0
        top = jnp.full((1, width), -jnp.inf, jnp.float32)
        for b in range(width // 128):
            lanes = pl.ds(b * 128, 128)
            t = share * ce_v[:, lanes].T + (1.0 - share) * cb_v[:, lanes].T
            t_acc[lanes, :] = t
            top = jnp.maximum(top, jnp.max(t, axis=0, keepdims=True))
        return top

    rows_at_once = 64
    blocks = width // rows_at_once

    def exp_sum(ref, top, scale):
        def body(b, total):
            rows = pl.ds(pl.multiple_of(b * rows_at_once, rows_at_once), rows_at_once)
            e = jnp.exp((ref[rows, :] - top) * scale)
            ref[rows, :] = e
            return total + jnp.sum(e.reshape(rows_at_once // 8, 8, width), axis=0)

        total = lax.fori_loop(0, blocks, body, jnp.zeros((8, width), jnp.float32))
        return jnp.sum(total, axis=0, keepdims=True)

    def put_stats(ref, top, total):
        for k in range(width // 128):
            ref[col, pl.ds(k, 1), :] = top[:, k * 128:(k + 1) * 128]
            ref[col, pl.ds(4 + k, 1), :] = total[:, k * 128:(k + 1) * 128]

    def send_stats(ref, which):
        def body(j, carry):
            k = 8 + ((j + 1) // 2) * (1 - 2 * (j % 2))
            to = (col + k) % 16
            remote(
                ref.at[col], ref.at[col], send_sem.at[7 + which], st_sem.at[which * 16 + k], (row, to)
            ).start()
            return carry

        lax.fori_loop(0, 15, body, 0)

    def wait_stats(ref, which):
        def body(k, carry):
            src = (col - k + 16) % 16
            remote(
                ref.at[src], ref.at[src], send_sem.at[7 + which], st_sem.at[which * 16 + k], (row, src)
            ).wait_recv()
            return carry

        lax.fori_loop(1, 16, body, 0)

    def combine(ref, scale):
        everyone = ref[...]
        tops, totals = everyone[:, 0:4, :], everyone[:, 4:8, :]
        top = jnp.max(tops, axis=0)
        total = jnp.sum(totals * jnp.exp((tops - top[None]) * scale), axis=0)
        mine = ref[col]
        return jnp.exp((mine[0:4, :] - top) * scale) / total

    arrives = {(p, to): (d, t) for d in range(4) for t, (p, _, to) in enumerate(GATHER_XY[d])}
    waited = set()

    def here(wait, d, t):
        if (wait, d, t) not in waited:
            waited.add((wait, d, t))
            wait(d, t)

    computed = 0
    for t in range(last_step + 1):
        for slot in range(4) if t == 0 else (t,) if 4 <= t < SLOTS_XY else ():
            for d in range(2):
                if slot >= 4:
                    here(gz_wait, d, GATHER_Z[d].index((GATHER_Z[d][slot][0] - 1, GATHER_Z[d][slot][1], False)))
                gz_copy(d, slot).start()
            for d in range(4):
                if slot >= 4:
                    here(gxy_wait, *arrives[GATHER_XY[d][slot][:2]])
                gxy_copy(d, slot).start()
        for d in range(2):
            if 0 <= t - LAG < SLOTS_Z:
                here(gz_wait, d, t - LAG)
        for d in range(4):
            if 0 <= t - LAG < SLOTS_XY:
                here(gxy_wait, d, t - LAG)
        if t == 0:
            remote(q_hbm, shard(q_all, col), send_sem.at[6], gpair_sem.at[4], pair_dev).start()
        if t == LAG:
            gpair_wait(0)
        for offset in range(1, 8):
            if z_steps[min(offset, 8 - offset)] + 1 == t:
                gpair_wait(offset)
        if t == 0:
            s_acc[...] = jnp.zeros_like(s_acc)
            t_top = teacher()
            t_total = exp_sum(t_acc, t_top, 1.0)
            put_stats(st_t, t_top, t_total)
        if t == last_step:
            send_stats(st_t, 1)
        if t == last_step:
            assert p_steps[4] == z_steps[4] + 1 == t > max(p_steps[:4] + p_steps[5:] + z_steps)
            first, second = row_from((2, 2)), z_at(4) * 2 + 1 - core
            add_chunk(first)

            @pl.when(first != second)
            def _():
                add_chunk(second)

        if t in (8, 11, 12, 13, 15, 16, 17):
            add_scores(computed, t)
            computed = t + 1

    def max_body(b, top):
        rows = pl.ds(pl.multiple_of(b * rows_at_once, rows_at_once), rows_at_once)
        return jnp.maximum(top, jnp.max(s_acc[rows, :].reshape(rows_at_once // 8, 8, width), axis=0))

    s_top = lax.fori_loop(0, blocks, max_body, jnp.full((8, width), -jnp.inf, jnp.float32))
    s_top = jnp.max(s_top, axis=0, keepdims=True)
    s_total = exp_sum(s_acc, s_top, 20.0)
    put_stats(st_s, s_top, s_total)
    send_stats(st_s, 0)

    wait_stats(st_t, 1)
    t_scale = combine(st_t, 1.0) * -20.0
    target = pos_ref[...] - col * width

    def teacher_body(b, carry):
        start = pl.multiple_of(b * rows_at_once, rows_at_once)
        rows = pl.ds(start, rows_at_once)
        scale = jnp.concatenate([t_scale[k:k + 1, :] for k in range(4)], axis=1)
        index = lax.broadcasted_iota(jnp.int32, (rows_at_once, width), 0) + start
        t_acc[rows, :] = t_acc[rows, :] * scale - jnp.where(index == target, 10.0, 0.0)
        return carry

    lax.fori_loop(0, blocks, teacher_body, 0)

    wait_stats(st_s, 0)
    s_scale = combine(st_s, 20.0) * 30.0

    def grad_body(b, carry):
        rows = pl.ds(pl.multiple_of(b * rows_at_once, rows_at_once), rows_at_once)
        scale = jnp.concatenate([s_scale[k:k + 1, :] for k in range(4)], axis=1)
        gs_t[rows, :] = (s_acc[rows, :] * scale + t_acc[rows, :]).astype(jnp.bfloat16)
        return carry

    lax.fori_loop(0, blocks, grad_body, 0)

    def query_part(offset, core_of):
        lhs = shard(p_all, z_at(offset) * 2 + core_of)[...]
        return jnp.dot(lhs, gs_t[...], preferred_element_type=jnp.float32)

    def pair_copies(offset):
        if offset != 4:
            whole = pair_out.at[offset], pair_in.at[offset]
            return [remote(*whole, send_sem.at[15], rpair_sem.at[offset], pair_dev)]
        return [
            remote(
                pair_out.at[4, pl.ds(u * unit, unit)], pair_in.at[4, pl.ds(u * unit, unit)],
                send_sem.at[15], rpair_sem.at[4 + 4 * at], pair_dev,
            )
            for at, u in enumerate(FAR_PAIR)
        ]

    def query_pair(offset):
        pair_out[offset] = query_part(offset, 1 - core).astype(jnp.bfloat16)
        for copy in pair_copies(offset):
            copy.start()

    def query_own(offset):
        qg_acc[offset] = query_part(offset, core)

    paired = set()

    passage_done = set()

    def passage_part(off):
        if off not in passage_done:
            passage_done.add(off)
            lhs = shard(q_all, row_from(off))[...]
            pg_acc[OFFSETS.index(off)] = lax.dot_general(
                lhs, gs_t[...], (((1,), (1,)), ((), ())), preferred_element_type=jnp.float32
            )

    def rxy_copy(d, t):
        return remote(
            xy_out.at[d * SLOTS_XY + t], xy_in.at[d * SLOTS_XY + t], send_sem.at[9 + d],
            rxy_sem.at[d * SLOTS_XY + t], xy_dev[d],
        )

    def xy_sum(p, off):
        total = pg_acc[OFFSETS.index(off), pl.ds(p * unit, unit), :]
        for d in range(4):
            for t, (p2, _, to) in enumerate(REDUCE_XY[d]):
                if p2 == p and to == off:
                    rxy_copy(d, t).wait_recv()
                    total += xy_in[d * SLOTS_XY + t].astype(jnp.float32)
        return total

    def rz_copy(d, t):
        _, u, cross = REDUCE_Z[d][t]
        src = pair_out.at[4, pl.ds(u * unit, unit)] if cross else z_out.at[d * SLOTS_Z + t]
        dev = cross_dev[d] if cross else z_dev[d]
        return remote(src, z_in.at[d * SLOTS_Z + t], send_sem.at[13 + d], rz_sem.at[d * SLOTS_Z + t], dev)

    def z_sum(directions, k, u):
        offset = (k if directions[0] == 0 else 8 - k) % 8
        rows = pl.ds(u * unit, unit)
        total = qg_acc[offset, rows, :]
        if k < 4:
            if offset not in paired:
                paired.add(offset)
                pair_copies(offset)[0].wait_recv()
            total += pair_in[offset, rows, :].astype(jnp.float32)
        elif u == FAR_PAIR[directions[0]]:
            pair_copies(4)[directions[0]].wait_recv()
            total += pair_in[offset, rows, :].astype(jnp.float32)
        for d in directions:
            for t, (k2, u2, _) in enumerate(REDUCE_Z[d]):
                if (k2, u2) == (k + 1, u):
                    rz_copy(d, t).wait_recv()
                    total += z_in[d * SLOTS_Z + t].astype(jnp.float32)
        return total

    for t in range(SLOTS_XY):
        for d in range(4):
            p, off, _ = REDUCE_XY[d][t]
            passage_part(off)
            xy_out[d * SLOTS_XY + t] = xy_sum(p, off).astype(jnp.bfloat16)
            rxy_copy(d, t).start()
        if t == 0:
            query_own(4)
        for d in range(2):
            k, u, cross = REDUCE_Z[d][t]
            if not cross:
                z_out[d * SLOTS_Z + t] = z_sum((d,), k, u).astype(jnp.bfloat16)
            rz_copy(d, t).start()
        if t == 0:
            query_pair(4)
        if t == 12:
            passage_part((0, 0))
        for at, offset in ((1, 3), (1, 5), (4, 2), (4, 6), (8, 1), (8, 7), (11, 0)):
            if t == at:
                query_pair(offset)
            if t == at + 1:
                query_own(offset)
    for u in range(PIECES):
        rows = pl.ds(u * unit, unit)
        out_ref[pl.ds(depth + u * unit, unit), :] = xy_sum(u, (0, 0)).astype(jnp.bfloat16)
        out_ref[rows, :] = z_sum((0, 1), 0, u).astype(jnp.bfloat16)

    def sent(ref, sem, dev):
        remote(ref, ref, sem, sem, dev).wait_send()

    for d in range(4):
        sent(p_all.at[pl.ds(0, SLOTS_XY * unit)], send_sem.at[d], xy_dev[d])
        sent(xy_out.at[pl.ds(d * SLOTS_XY, SLOTS_XY)], send_sem.at[9 + d], xy_dev[d])
    for d in range(2):
        sent(q_all.at[pl.ds(0, SLOTS_Z * unit)], send_sem.at[4 + d], z_dev[d])
        sent(z_out.at[pl.ds(d * SLOTS_Z, SLOTS_Z)], send_sem.at[13 + d], z_dev[d])
    sent(q_all.at[pl.ds(0, 30 * unit)], send_sem.at[6], pair_dev)
    sent(q_all.at[pl.ds(0, 30 * unit)], send_sem.at[15], pair_dev)
    sent(st_s.at[pl.ds(0, 15)], send_sem.at[7], pair_dev)
    sent(st_t.at[pl.ds(0, 15)], send_sem.at[8], pair_dev)


def per_device(queries, passages, ce_scores, colbert_scores, mix, positive):
    depth, width = queries.shape
    unit = depth // PIECES
    bf16, f32 = jnp.bfloat16, jnp.float32
    hbm = pl.BlockSpec(memory_space=pl.ANY)
    vmem = pl.BlockSpec(memory_space=pltpu.VMEM)
    out = pltpu.VMEM((2 * depth, width), bf16)
    dma = pltpu.SemaphoreType.DMA
    grads = pl.pallas_call(
        kernel,
        out_shape=out,
        in_specs=[hbm] * 6,
        out_specs=vmem,
        scratch_shapes=[
            pltpu.VMEM((16 * depth, width), bf16),
            pltpu.VMEM((16 * depth, width), bf16),
            pltpu.VMEM((width, width), f32),
            pltpu.VMEM((width, width), f32),
            pltpu.VMEM((1, width), jnp.int32),
            pltpu.VMEM((1, width), jnp.int32),
            pltpu.VMEM((width, width), f32),
            pltpu.VMEM((width, width), f32),
            pltpu.VMEM((width, width), bf16),
            pltpu.VMEM((16, 8, 128), f32),
            pltpu.VMEM((16, 8, 128), f32),
            pltpu.VMEM((16, depth, width), f32),
            pltpu.VMEM((8, depth, width), f32),
            pltpu.VMEM((8, depth, width), bf16),
            pltpu.VMEM((8, depth, width), bf16),
            pltpu.VMEM((4 * SLOTS_XY, unit, width), bf16),
            pltpu.VMEM((4 * SLOTS_XY, unit, width), bf16),
            pltpu.VMEM((2 * SLOTS_Z, unit, width), bf16),
            pltpu.VMEM((2 * SLOTS_Z, unit, width), bf16),
            dma((6,)),
            dma((16,)),
            dma((4 * SLOTS_XY,)),
            dma((2 * SLOTS_Z,)),
            dma((9,)),
            dma((32,)),
            dma((4 * SLOTS_XY,)),
            dma((2 * SLOTS_Z,)),
            dma((9,)),
        ],
        compiler_params=pltpu.CompilerParams(collective_id=0, has_side_effects=True),
    )(queries, passages, ce_scores, colbert_scores, mix.reshape(1, width), positive.reshape(1, width))
    return grads[:depth], grads[depth:]


def solution(mesh):
    in_specs = (
        P("col", "row"),
        P("row", "col"),
        P("row", "col"),
        P("row", "col"),
        P("row"),
        P("row"),
    )
    out_specs = (P("col", "row"), P("row", "col"))
    return jax.shard_map(
        per_device, mesh=mesh, in_specs=in_specs, out_specs=out_specs, check_vma=False
    )
```

```python
import functools

import jax
import jax.numpy as jnp
from jax import lax
from jax.experimental import pallas as pl
from jax.experimental.pallas import tpu as pltpu
from jax.sharding import PartitionSpec as P

MESH = pl.DeviceIdType.MESH
DELTA = ((1, 0), (0, 1), (-1, 0), (0, -1))
LAG = 4
PIECES = 4


def far(offset):
    return sum(min(o, 4 - o) for o in offset)


def group(offset):
    two_x, two_y = offset[0] == 2, offset[1] == 2
    if far(offset) == 3:
        return 5 if two_x else 3
    return 6 if far(offset) == 2 and (two_x or two_y) else far(offset)


TURNS = {(2, 0): 0, (0, 2): 0, (1, 1): 1, (3, 3): 1, (3, 1): 2, (1, 3): 2, (1, 2): 0, (3, 2): 0, (2, 1): 1, (2, 3): 1}


def tree_edges(piece):
    base = [((0, 0), 0), ((1, 0), 0), ((0, 0), 2)]
    for x in range(4):
        base += [((x, 0), 1), ((x, 1), 1), ((x, 0), 3)]
    edges = []
    for (x, y), direction in base:
        for _ in range(piece):
            x, y = -y, x
        direction = (direction + piece) % 4
        dx, dy = DELTA[direction]
        edges.append(((x % 4, y % 4), direction, ((x + dx) % 4, (y + dy) % 4)))
    return edges


def xy_schedule():
    trees = [tree_edges(piece) for piece in range(PIECES)]

    def late(piece, node):
        return far(node) == 3 and all(start != node for start, _, _ in trees[piece])

    ready = {(piece, (0, 0)): 0 for piece in range(PIECES)}
    left = {(piece,) + edge for piece in range(PIECES) for edge in trees[piece]}
    plan = [[] for _ in range(4)]
    slot = 0
    while left:
        taken = []
        for direction in range(4):
            able = [e for e in left if e[2] == direction and ready.get((e[0], e[1]), 99) <= slot]
            if able:
                able.sort(key=lambda e: (far(e[3]), late(e[0], e[3]), TURNS.get(e[3], (0, 2, 3, 1)[(e[0] - direction) % 4])))
                taken.append(able[0])
        for piece, start, direction, to in taken:
            left.remove((piece, start, direction, to))
            plan[direction].append((piece, start, to))
            ready[piece, to] = slot + LAG
        slot += 1
    return plan


GATHER_XY = xy_schedule()
REDUCE_XY = [[(p, to, start) for p, start, to in reversed(GATHER_XY[(d + 2) % 4])] for d in range(4)]
HALVES = ((0, 1, 2, 3), (2, 3, 0, 1))
GATHER_Z = [
    [(k, u, False) for k in range(3) for u in h] + [(3, h[0], False), (3, h[1], False), (3, h[1], True)]
    for h in HALVES
]
REDUCE_Z = [
    [(4, h[1], False), (4, h[1], True), (4, h[0], False)]
    + [(k, u, False) for k in (3, 2, 1) for u in (h[2], h[3], h[1], h[0])]
    for h in HALVES
]
FAR_PAIR = [h[0] for h in HALVES]
SLOTS_XY = len(GATHER_XY[0])
SLOTS_Z = len(GATHER_Z[0])
OFFSETS = [(x, y) for x in range(4) for y in range(4)]


def pick(index, values):
    out = jnp.int32(values[0])
    for at, value in enumerate(values[1:], 1):
        out = jnp.where(index == at, jnp.int32(value), out)
    return out


def kernel(
    q_hbm, p_hbm, ce_hbm, cb_hbm, mix_hbm, pos_hbm,
    out_ref,
    q_all, p_all, ce_v, cb_v, mix_ref, pos_ref, s_acc, t_acc, gs_t, st_s, st_t,
    pg_acc, qg_acc, pair_out, pair_in, xy_out, xy_in, z_out, z_in,
    local_sem, send_sem, gxy_sem, gz_sem, gpair_sem, st_sem, rxy_sem, rz_sem, rpair_sem,
):
    row, col = lax.axis_index("row"), lax.axis_index("col")
    x, y, z, core = row // 4, row % 4, col // 2, col % 2
    depth, width = q_hbm.shape
    unit = depth // PIECES

    def row_at(dx, dy):
        return ((x + dx + 4) % 4) * 4 + (y + dy + 4) % 4

    def z_at(dz):
        return (z + dz + 8) % 8

    xy_dev = [(row_at(dx, dy), col) for dx, dy in DELTA]
    z_dev = [(row, z_at(1) * 2 + core), (row, z_at(-1) * 2 + core)]
    cross_dev = [(row, z_at(1) * 2 + 1 - core), (row, z_at(-1) * 2 + 1 - core)]
    pair_dev = (row, z * 2 + 1 - core)

    def shard(ref, index):
        return ref.at[pl.ds(pl.multiple_of(index * depth, depth), depth)]

    def piece(ref, index, u):
        return ref.at[pl.ds(pl.multiple_of(index * depth + u * unit, unit), unit)]

    def remote(src, dst, ssem, rsem, dev):
        return pltpu.make_async_remote_copy(
            src_ref=src, dst_ref=dst, send_sem=ssem, recv_sem=rsem, device_id=dev, device_id_type=MESH
        )

    barrier = pltpu.get_barrier_semaphore()
    for dev in xy_dev + z_dev + [pair_dev]:
        pl.semaphore_signal(barrier, inc=1, device_id=dev, device_id_type=MESH)
    loads = [
        pltpu.make_async_copy(src, dst, local_sem.at[at])
        for at, (src, dst) in enumerate(
            (
                (q_hbm, shard(q_all, col)),
                (p_hbm, shard(p_all, row)),
                (ce_hbm, ce_v),
                (cb_hbm, cb_v),
                (mix_hbm, mix_ref),
                (pos_hbm, pos_ref),
            )
        )
    ]
    for load in loads:
        load.start()
    pl.semaphore_wait(barrier, 7)

    def row_from(off):
        return row_at(-off[0], -off[1])

    def gxy_copy(d, t):
        p, start, _ = GATHER_XY[d][t]
        ref = piece(p_all, row_from(start), p)
        src = p_hbm.at[pl.ds(p * unit, unit)] if start == (0, 0) else ref
        return remote(src, ref, send_sem.at[d], gxy_sem.at[d * SLOTS_XY + t], xy_dev[d])

    def gxy_wait(d, t):
        p, _, to = GATHER_XY[d][t]
        ref = piece(p_all, row_from(to), p)
        remote(ref, ref, send_sem.at[d], gxy_sem.at[d * SLOTS_XY + t], xy_dev[d]).wait_recv()

    def z_from(d, k, core_of):
        return z_at(-k if d == 0 else k) * 2 + core_of

    def gz_copy(d, t):
        k, u, cross = GATHER_Z[d][t]
        ref = piece(q_all, z_from(d, k, core), u)
        src = q_hbm.at[pl.ds(u * unit, unit)] if k == 0 else ref
        dev = cross_dev[d] if cross else z_dev[d]
        return remote(src, ref, send_sem.at[4 + d], gz_sem.at[d * SLOTS_Z + t], dev)

    def gz_wait(d, t):
        k, u, cross = GATHER_Z[d][t]
        ref = piece(q_all, z_from(d, k + 1, 1 - core if cross else core), u)
        dev = cross_dev[d] if cross else z_dev[d]
        remote(ref, ref, send_sem.at[4 + d], gz_sem.at[d * SLOTS_Z + t], dev).wait_recv()
        offset = (k + 1) if d == 1 else (8 - k - 1)
        if k < 3:
            remote(ref, ref, send_sem.at[6], gpair_sem.at[offset], pair_dev).start()
        elif u == FAR_PAIR[d]:
            remote(ref, ref, send_sem.at[6], gpair_sem.at[8 * d], pair_dev).start()

    def gpair_wait(offset):
        other = z_at(offset) * 2 + 1 - core
        if offset == 4:
            for d in range(2):
                ref = piece(q_all, other, FAR_PAIR[d])
                remote(ref, ref, send_sem.at[6], gpair_sem.at[8 * d], pair_dev).wait_recv()
        else:
            ref = shard(q_all, other)
            at = 4 if offset == 0 else offset
            remote(ref, ref, send_sem.at[6], gpair_sem.at[at], pair_dev).wait_recv()

    last_step = SLOTS_XY + LAG - 1
    p_steps = [0] * 7
    for d in range(4):
        for t, (_, _, to) in enumerate(GATHER_XY[d]):
            p_steps[group(to)] = max(p_steps[group(to)], t + LAG)
    z_steps = [0] * 5
    for d in range(2):
        for t, (k, _, cross) in enumerate(GATHER_Z[d]):
            z_steps[k + 1] = max(z_steps[k + 1], t + LAG - (1 if cross else 0))


    def add_chunk(i):
        start = pl.multiple_of(i * depth, depth)
        s_acc[...] += lax.dot_general(
            p_all[pl.ds(start, depth), :],
            q_all[pl.ds(start, depth), :],
            (((0,), (0,)), ((), ())),
            preferred_element_type=jnp.float32,
        )

    def add_scores(lo, hi):
        def body(i, carry):
            dx, dy, dz = jnp.abs(x - i // 4), jnp.abs(y - i % 4), jnp.abs(z - i // 2)
            dx, dy = jnp.minimum(dx, 4 - dx), jnp.minimum(dy, 4 - dy)
            p_far = dx + dy
            two = jnp.where(p_far == 2, jnp.maximum(dx, dy), 0) == 2
            p_far = jnp.where(two, 6, jnp.where(jnp.where(p_far == 3, dx, 0) == 2, 5, p_far))
            z_far = jnp.minimum(dz, 8 - dz)
            other = jnp.where(i % 2 == core, 0, 1)
            at = jnp.maximum(pick(p_far, p_steps), pick(z_far, z_steps) + other)

            @pl.when(jnp.logical_and(at >= lo, at <= hi))
            def _():
                add_chunk(i)

            return carry

        lax.fori_loop(0, 16, body, 0)

    def teacher():
        for load in loads:
            load.wait()
        share = mix_ref[...].astype(jnp.float32) / 256.0
        top = jnp.full((1, width), -jnp.inf, jnp.float32)
        for b in range(width // 128):
            lanes = pl.ds(b * 128, 128)
            t = share * ce_v[:, lanes].T + (1.0 - share) * cb_v[:, lanes].T
            t_acc[lanes, :] = t
            top = jnp.maximum(top, jnp.max(t, axis=0, keepdims=True))
        return top

    rows_at_once = 64
    blocks = width // rows_at_once

    def exp_sum(ref, top, scale):
        def body(b, total):
            rows = pl.ds(pl.multiple_of(b * rows_at_once, rows_at_once), rows_at_once)
            e = jnp.exp((ref[rows, :] - top) * scale)
            ref[rows, :] = e
            return total + jnp.sum(e.reshape(rows_at_once // 8, 8, width), axis=0)

        total = lax.fori_loop(0, blocks, body, jnp.zeros((8, width), jnp.float32))
        return jnp.sum(total, axis=0, keepdims=True)

    def put_stats(ref, top, total):
        for k in range(width // 128):
            ref[col, pl.ds(k, 1), :] = top[:, k * 128:(k + 1) * 128]
            ref[col, pl.ds(4 + k, 1), :] = total[:, k * 128:(k + 1) * 128]

    def send_stats(ref, which, lo, hi):
        def body(j, carry):
            k = 8 + ((j + 1) // 2) * (1 - 2 * (j % 2))
            to = (col + k) % 16
            remote(
                ref.at[col], ref.at[col], send_sem.at[7 + which], st_sem.at[which * 16 + k], (row, to)
            ).start()
            return carry

        lax.fori_loop(lo, hi, body, 0)

    def wait_stats(ref, which):
        def body(k, carry):
            src = (col - k + 16) % 16
            remote(
                ref.at[src], ref.at[src], send_sem.at[7 + which], st_sem.at[which * 16 + k], (row, src)
            ).wait_recv()
            return carry

        lax.fori_loop(1, 16, body, 0)

    def combine(ref, scale):
        everyone = ref[...]
        tops, totals = everyone[:, 0:4, :], everyone[:, 4:8, :]
        top = jnp.max(tops, axis=0)
        total = jnp.sum(totals * jnp.exp((tops - top[None]) * scale), axis=0)
        mine = ref[col]
        return jnp.exp((mine[0:4, :] - top) * scale) / total

    arrives = {(p, to): (d, t) for d in range(4) for t, (p, _, to) in enumerate(GATHER_XY[d])}
    waited = set()

    def here(wait, d, t):
        if (wait, d, t) not in waited:
            waited.add((wait, d, t))
            wait(d, t)

    computed = 0
    for t in range(last_step + 1):
        for slot in range(4) if t == 0 else (t,) if 4 <= t < SLOTS_XY else ():
            for d in range(2):
                if slot >= 4:
                    here(gz_wait, d, GATHER_Z[d].index((GATHER_Z[d][slot][0] - 1, GATHER_Z[d][slot][1], False)))
                gz_copy(d, slot).start()
            for d in range(4):
                if slot >= 4:
                    here(gxy_wait, *arrives[GATHER_XY[d][slot][:2]])
                gxy_copy(d, slot).start()
        for d in range(2):
            if 0 <= t - LAG < SLOTS_Z:
                here(gz_wait, d, t - LAG)
        for d in range(4):
            if 0 <= t - LAG < SLOTS_XY:
                here(gxy_wait, d, t - LAG)
        if t == 0:
            remote(q_hbm, shard(q_all, col), send_sem.at[6], gpair_sem.at[4], pair_dev).start()
        if t == LAG:
            gpair_wait(0)
        for offset in range(1, 8):
            if z_steps[min(offset, 8 - offset)] + 1 == t:
                gpair_wait(offset)
        if t == 0:
            s_acc[...] = jnp.zeros_like(s_acc)
            t_top = teacher()
            t_total = exp_sum(t_acc, t_top, 1.0)
            put_stats(st_t, t_top, t_total)
        if t == last_step:
            send_stats(st_t, 1, 0, 3)
        if t == last_step:
            assert p_steps[4] == z_steps[4] + 1 == t > max(p_steps[:4] + p_steps[5:] + z_steps)
            first, second = row_from((2, 2)), z_at(4) * 2 + 1 - core
            add_chunk(first)

            @pl.when(first != second)
            def _():
                add_chunk(second)

        if t in (8, 11, 12, 13, 15, 16, 17):
            add_scores(computed, t)
            computed = t + 1

    def max_body(b, top):
        rows = pl.ds(pl.multiple_of(b * rows_at_once, rows_at_once), rows_at_once)
        return jnp.maximum(top, jnp.max(s_acc[rows, :].reshape(rows_at_once // 8, 8, width), axis=0))

    s_top = lax.fori_loop(0, blocks, max_body, jnp.full((8, width), -jnp.inf, jnp.float32))
    s_top = jnp.max(s_top, axis=0, keepdims=True)
    s_total = exp_sum(s_acc, s_top, 20.0)
    put_stats(st_s, s_top, s_total)
    send_stats(st_s, 0, 0, 15)
    send_stats(st_t, 1, 3, 15)

    wait_stats(st_t, 1)
    t_scale = combine(st_t, 1.0) * -20.0
    target = pos_ref[...] - col * width

    def teacher_body(b, carry):
        start = pl.multiple_of(b * rows_at_once, rows_at_once)
        rows = pl.ds(start, rows_at_once)
        scale = jnp.concatenate([t_scale[k:k + 1, :] for k in range(4)], axis=1)
        index = lax.broadcasted_iota(jnp.int32, (rows_at_once, width), 0) + start
        t_acc[rows, :] = t_acc[rows, :] * scale - jnp.where(index == target, 10.0, 0.0)
        return carry

    lax.fori_loop(0, blocks, teacher_body, 0)

    wait_stats(st_s, 0)
    s_scale = combine(st_s, 20.0) * 30.0

    def grad_body(b, carry):
        rows = pl.ds(pl.multiple_of(b * rows_at_once, rows_at_once), rows_at_once)
        scale = jnp.concatenate([s_scale[k:k + 1, :] for k in range(4)], axis=1)
        gs_t[rows, :] = (s_acc[rows, :] * scale + t_acc[rows, :]).astype(jnp.bfloat16)
        return carry

    lax.fori_loop(0, blocks, grad_body, 0)

    def query_part(offset, core_of):
        lhs = shard(p_all, z_at(offset) * 2 + core_of)[...]
        return jnp.dot(lhs, gs_t[...], preferred_element_type=jnp.float32)

    def pair_copies(offset):
        if offset != 4:
            whole = pair_out.at[offset], pair_in.at[offset]
            return [remote(*whole, send_sem.at[15], rpair_sem.at[offset], pair_dev)]
        return [
            remote(
                pair_out.at[4, pl.ds(u * unit, unit)], pair_in.at[4, pl.ds(u * unit, unit)],
                send_sem.at[15], rpair_sem.at[4 + 4 * at], pair_dev,
            )
            for at, u in enumerate(FAR_PAIR)
        ]

    def query_pair(offset):
        pair_out[offset] = query_part(offset, 1 - core).astype(jnp.bfloat16)
        for copy in pair_copies(offset):
            copy.start()

    def query_own(offset):
        qg_acc[offset] = query_part(offset, core)

    paired = set()

    passage_done = set()

    def passage_part(off):
        if off not in passage_done:
            passage_done.add(off)
            lhs = shard(q_all, row_from(off))[...]
            pg_acc[OFFSETS.index(off)] = lax.dot_general(
                lhs, gs_t[...], (((1,), (1,)), ((), ())), preferred_element_type=jnp.float32
            )

    def rxy_copy(d, t):
        return remote(
            xy_out.at[d * SLOTS_XY + t], xy_in.at[d * SLOTS_XY + t], send_sem.at[9 + d],
            rxy_sem.at[d * SLOTS_XY + t], xy_dev[d],
        )

    def xy_sum(p, off):
        total = pg_acc[OFFSETS.index(off), pl.ds(p * unit, unit), :]
        for d in range(4):
            for t, (p2, _, to) in enumerate(REDUCE_XY[d]):
                if p2 == p and to == off:
                    rxy_copy(d, t).wait_recv()
                    total += xy_in[d * SLOTS_XY + t].astype(jnp.float32)
        return total

    def rz_copy(d, t):
        _, u, cross = REDUCE_Z[d][t]
        src = pair_out.at[4, pl.ds(u * unit, unit)] if cross else z_out.at[d * SLOTS_Z + t]
        dev = cross_dev[d] if cross else z_dev[d]
        return remote(src, z_in.at[d * SLOTS_Z + t], send_sem.at[13 + d], rz_sem.at[d * SLOTS_Z + t], dev)

    def z_sum(directions, k, u):
        offset = (k if directions[0] == 0 else 8 - k) % 8
        rows = pl.ds(u * unit, unit)
        total = qg_acc[offset, rows, :]
        if k < 4:
            if offset not in paired:
                paired.add(offset)
                pair_copies(offset)[0].wait_recv()
            total += pair_in[offset, rows, :].astype(jnp.float32)
        elif u == FAR_PAIR[directions[0]]:
            pair_copies(4)[directions[0]].wait_recv()
            total += pair_in[offset, rows, :].astype(jnp.float32)
        for d in directions:
            for t, (k2, u2, _) in enumerate(REDUCE_Z[d]):
                if (k2, u2) == (k + 1, u):
                    rz_copy(d, t).wait_recv()
                    total += z_in[d * SLOTS_Z + t].astype(jnp.float32)
        return total

    for t in range(SLOTS_XY):
        for d in range(4):
            p, off, _ = REDUCE_XY[d][t]
            passage_part(off)
            xy_out[d * SLOTS_XY + t] = xy_sum(p, off).astype(jnp.bfloat16)
            rxy_copy(d, t).start()
        if t == 0:
            query_own(4)
        for d in range(2):
            k, u, cross = REDUCE_Z[d][t]
            if not cross:
                z_out[d * SLOTS_Z + t] = z_sum((d,), k, u).astype(jnp.bfloat16)
            rz_copy(d, t).start()
        if t == 0:
            query_pair(4)
        if t == 12:
            passage_part((0, 0))
        for at, offset in ((1, 3), (1, 5), (4, 2), (4, 6), (8, 1), (8, 7), (11, 0)):
            if t == at:
                query_pair(offset)
            if t == at + 1:
                query_own(offset)
    for u in range(PIECES):
        rows = pl.ds(u * unit, unit)
        out_ref[pl.ds(depth + u * unit, unit), :] = xy_sum(u, (0, 0)).astype(jnp.bfloat16)
        out_ref[rows, :] = z_sum((0, 1), 0, u).astype(jnp.bfloat16)

    def sent(ref, sem, dev):
        remote(ref, ref, sem, sem, dev).wait_send()

    for d in range(4):
        sent(p_all.at[pl.ds(0, SLOTS_XY * unit)], send_sem.at[d], xy_dev[d])
        sent(xy_out.at[pl.ds(d * SLOTS_XY, SLOTS_XY)], send_sem.at[9 + d], xy_dev[d])
    for d in range(2):
        sent(q_all.at[pl.ds(0, SLOTS_Z * unit)], send_sem.at[4 + d], z_dev[d])
        sent(z_out.at[pl.ds(d * SLOTS_Z, SLOTS_Z)], send_sem.at[13 + d], z_dev[d])
    sent(q_all.at[pl.ds(0, 30 * unit)], send_sem.at[6], pair_dev)
    sent(q_all.at[pl.ds(0, 30 * unit)], send_sem.at[15], pair_dev)
    sent(st_s.at[pl.ds(0, 15)], send_sem.at[7], pair_dev)
    sent(st_t.at[pl.ds(0, 15)], send_sem.at[8], pair_dev)


def per_device(queries, passages, ce_scores, colbert_scores, mix, positive):
    depth, width = queries.shape
    unit = depth // PIECES
    bf16, f32 = jnp.bfloat16, jnp.float32
    hbm = pl.BlockSpec(memory_space=pl.ANY)
    vmem = pl.BlockSpec(memory_space=pltpu.VMEM)
    out = pltpu.VMEM((2 * depth, width), bf16)
    dma = pltpu.SemaphoreType.DMA
    grads = pl.pallas_call(
        kernel,
        out_shape=out,
        in_specs=[hbm] * 6,
        out_specs=vmem,
        scratch_shapes=[
            pltpu.VMEM((16 * depth, width), bf16),
            pltpu.VMEM((16 * depth, width), bf16),
            pltpu.VMEM((width, width), f32),
            pltpu.VMEM((width, width), f32),
            pltpu.VMEM((1, width), jnp.int32),
            pltpu.VMEM((1, width), jnp.int32),
            pltpu.VMEM((width, width), f32),
            pltpu.VMEM((width, width), f32),
            pltpu.VMEM((width, width), bf16),
            pltpu.VMEM((16, 8, 128), f32),
            pltpu.VMEM((16, 8, 128), f32),
            pltpu.VMEM((16, depth, width), f32),
            pltpu.VMEM((8, depth, width), f32),
            pltpu.VMEM((8, depth, width), bf16),
            pltpu.VMEM((8, depth, width), bf16),
            pltpu.VMEM((4 * SLOTS_XY, unit, width), bf16),
            pltpu.VMEM((4 * SLOTS_XY, unit, width), bf16),
            pltpu.VMEM((2 * SLOTS_Z, unit, width), bf16),
            pltpu.VMEM((2 * SLOTS_Z, unit, width), bf16),
            dma((6,)),
            dma((16,)),
            dma((4 * SLOTS_XY,)),
            dma((2 * SLOTS_Z,)),
            dma((9,)),
            dma((32,)),
            dma((4 * SLOTS_XY,)),
            dma((2 * SLOTS_Z,)),
            dma((9,)),
        ],
        compiler_params=pltpu.CompilerParams(collective_id=0, has_side_effects=True),
    )(queries, passages, ce_scores, colbert_scores, mix.reshape(1, width), positive.reshape(1, width))
    return grads[:depth], grads[depth:]


def solution(mesh):
    in_specs = (
        P("col", "row"),
        P("row", "col"),
        P("row", "col"),
        P("row", "col"),
        P("row"),
        P("row"),
    )
    out_specs = (P("col", "row"), P("row", "col"))
    return jax.shard_map(
        per_device, mesh=mesh, in_specs=in_specs, out_specs=out_specs, check_vma=False
    )
```
